32 devices in a mesh: wide: 16 (over z, y, x), narrow: 2 (over core).
Axes of the slice: x: 2, y: 2, z: 4, core: 2. Of those that a mesh axis runs over, the one named last changes fastest.
Arguments:
- tokens: bfloat16 [32, 8192], P('wide', 'narrow'), may hold values from -6 to 6
- cotangent: bfloat16 [32, 8192], P('wide', 'narrow'), may hold values from -6 to 6
- gate_tiles: bfloat16 [2, 16, 48, 128, 128], P('narrow', 'wide'), may hold values from -0.109375 to 0.109375
- up_tiles: bfloat16 [2, 16, 48, 128, 128], P('narrow', 'wide'), may hold values from -0.109375 to 0.109375
- down_tiles: bfloat16 [2, 16, 48, 128, 128], P('narrow', 'wide'), may hold values from -0.125 to 0.125
- kept_slots: int32 [3, 2, 16, 48], P(None, 'narrow', 'wide'), may hold values from 0 to 95, as said below
- kept_counts: int32 [3, 2, 16], P(None, 'narrow', 'wide'), may hold values from 12 to 48, as said below
Outputs:
- layer_out: bfloat16 [32, 8192], P('wide', 'narrow')
- input_grad: bfloat16 [32, 8192], P('wide', 'narrow')
- gate_grad: bfloat16 [2, 16, 48, 128, 128], P('narrow', 'wide')
- up_grad: bfloat16 [2, 16, 48, 128, 128], P('narrow', 'wide')
- down_grad: bfloat16 [2, 16, 48, 128, 128], P('narrow', 'wide')
The draws below stay inside these ranges and needn't reach their ends.
Inputs may be any that keep to these rules, and one draw needn't show every extreme that they name: `kept_slots`: for each matrix and device the first 48 entries are distinct local tile positions. `kept_counts`: for each matrix some device keeps exactly 48 tiles.
All inputs are finite; a program needn't handle non-finite values.
Results may differ from the reference program's by a relative error of at most 0.005.
Values may be sent and summed in bfloat16 or wider, within the bound.
No kernel may reach another device: no remote copies, remote signals or barrier semaphores. Data moves between devices by JAX's collectives and lax.ppermute only.
A program may use at most 64 MiB of HBM per device.

```python
import jax
import jax.numpy as jnp
from jax import lax

D = 8192
TILE = 128
HT_DEV = 3
HIDDEN_SIZE = 6144
TOKENS = 32
DT_DEV = 32
LOC = 96
CAP = 48
N_WIDE = 16
N_NARROW = 2


def shuffle_positions(subkey):
    return jax.random.permutation(subkey, LOC)[:CAP]


def draw_kept_slots(key, part):
    subkeys = jax.random.split(jax.random.fold_in(key, 11), 3 * N_NARROW * N_WIDE)
    lists = jax.vmap(shuffle_positions)(subkeys)
    return lists.reshape(3, N_NARROW, N_WIDE, CAP).astype(jnp.int32)


def draw_kept_counts(key, part):
    lowest = max(LOC // 8, 1)
    spread = CAP - lowest + 1
    first = jax.random.randint(jax.random.fold_in(key, 21), (3, N_NARROW * N_WIDE), 0, spread)
    second = jax.random.randint(jax.random.fold_in(key, 22), (3, N_NARROW * N_WIDE), 0, spread)
    counts = lowest + jnp.minimum(first, second)
    chosen = jax.random.randint(jax.random.fold_in(key, 23), (3,), 0, N_NARROW * N_WIDE)
    counts = counts.at[jnp.arange(3), chosen].set(CAP)
    return counts.reshape(3, N_NARROW, N_WIDE).astype(jnp.int32)


def steps_of(key, extent, pieces, smallest, top_value):
    level, own = 1.0, jax.random.fold_in(key, 6)
    for dim, blocks in pieces:
        heights = jnp.exp(jax.random.uniform(jax.random.fold_in(own, dim), (blocks,), jnp.float32, smallest / len(pieces), top_value / len(pieces)))
        level = level * jnp.repeat(heights, extent[dim] // blocks).reshape([-1 if axis == dim else 1 for axis in range(len(extent))])
    return level


def noise(rng, shape, scale, limit, cuts=(), held_as=jnp.bfloat16):
    level = steps_of(rng, shape, cuts, -0.22, 0.18) if cuts else 1.0
    entries = jax.random.normal(rng, shape, jnp.float32) * scale * level
    return jnp.minimum(jnp.maximum(entries, -limit), limit).astype(held_as)


def setup_inputs(seed: int = 0) -> dict:
    key_of = jax.random.split(jax.random.key(seed), 8)
    tokens = noise(key_of[0], (TOKENS, D), 1.0, 6.0, ((0, 16), (1, 2)))
    cotangent = noise(key_of[1], (TOKENS, D), 1.0, 6.0, ((0, 16), (1, 2)))
    gate_tiles = noise(key_of[2], (N_NARROW, N_WIDE, CAP, TILE, TILE), (D // 3) ** -0.5, 0.109375, ((0, 2), (1, 16)))
    up_tiles = noise(key_of[3], (N_NARROW, N_WIDE, CAP, TILE, TILE), (D // 3) ** -0.5, 0.109375, ((0, 2), (1, 16)))
    down_tiles = noise(key_of[4], (N_NARROW, N_WIDE, CAP, TILE, TILE), (HIDDEN_SIZE // 3) ** -0.5, 0.125, ((0, 2), (1, 16)))
    kept_slots = draw_kept_slots(jax.random.fold_in(key_of[7], 71), 0)
    kept_counts = draw_kept_counts(jax.random.fold_in(key_of[7], 71), 0)
    return {"tokens": tokens, "cotangent": cotangent, "gate_tiles": gate_tiles, "up_tiles": up_tiles, "down_tiles": down_tiles, "kept_slots": kept_slots, "kept_counts": kept_counts}


highest = lax.Precision.HIGHEST

def onehots(slot_list, kept_count, row_tiles, col_tiles):
    row_onehot = (slot_list[:, None] // col_tiles == jnp.arange(row_tiles, dtype=jnp.int32)[None, :]).astype(jnp.float32)
    col_onehot = (slot_list[:, None] % col_tiles == jnp.arange(col_tiles, dtype=jnp.int32)[None, :]).astype(jnp.float32)
    live_mask = (jnp.arange(slot_list.shape[0], dtype=jnp.int32) < kept_count).astype(jnp.float32)
    return (row_onehot, col_onehot, live_mask)

def tile_product(panel_in, tiles, slot_list, kept_count, col_tiles):
    row_onehot, col_onehot, live_mask = onehots(slot_list, kept_count, panel_in.shape[1], col_tiles)
    picked = jnp.einsum('tra,kr->kta', panel_in.astype(jnp.float32), row_onehot, precision=highest)
    product = jnp.einsum('kta,kab->ktb', picked, tiles.astype(jnp.float32), precision=highest)
    return jnp.einsum('ktb,kc->tcb', product, col_onehot * live_mask[:, None], precision=highest)

def tile_transposed(panel_out, tiles, slot_list, kept_count, row_tiles):
    row_onehot, col_onehot, live_mask = onehots(slot_list, kept_count, row_tiles, panel_out.shape[1])
    picked = jnp.einsum('tcb,kc->ktb', panel_out.astype(jnp.float32), col_onehot, precision=highest)
    product = jnp.einsum('ktb,kab->kta', picked, tiles.astype(jnp.float32), precision=highest)
    return jnp.einsum('kta,kr->tra', product, row_onehot * live_mask[:, None], precision=highest)

def tile_grad(panel_in, panel_out, slot_list, kept_count):
    row_onehot, col_onehot, live_mask = onehots(slot_list, kept_count, panel_in.shape[1], panel_out.shape[1])
    picked_in = jnp.einsum('tra,kr->kta', panel_in.astype(jnp.float32), row_onehot, precision=highest)
    picked_out = jnp.einsum('tcb,kc->ktb', panel_out.astype(jnp.float32), col_onehot, precision=highest)
    grads = jnp.einsum('kta,ktb->kab', picked_in, picked_out, precision=highest)
    return (grads * live_mask[:, None, None]).astype(jnp.bfloat16)

def reference(tokens, cotangent, gate_tiles, up_tiles, down_tiles, kept_slots, kept_counts):
    token_blocks = tokens.reshape(TOKENS, N_NARROW, DT_DEV, TILE).transpose(1, 0, 2, 3)
    grad_blocks = cotangent.reshape(TOKENS, N_NARROW, DT_DEV, TILE).transpose(1, 0, 2, 3)

    def gate_column(wide_index):

        def single(narrow_index):
            first = tile_product(token_blocks[narrow_index], gate_tiles[narrow_index, wide_index], kept_slots[0, narrow_index, wide_index], kept_counts[0, narrow_index, wide_index], HT_DEV)
            second = tile_product(token_blocks[narrow_index], up_tiles[narrow_index, wide_index], kept_slots[1, narrow_index, wide_index], kept_counts[1, narrow_index, wide_index], HT_DEV)
            return (first, second)
        firsts, seconds = jax.vmap(single)(jnp.arange(N_NARROW))
        return (lax.optimization_barrier(jnp.sum(firsts, 0)), lax.optimization_barrier(jnp.sum(seconds, 0)))
    gate_sum, up_sum = lax.map(gate_column, jnp.arange(N_WIDE))
    hidden = (jax.nn.silu(gate_sum) * up_sum).astype(jnp.bfloat16)

    def out_block(narrow_index):

        def accumulate(wide_index, carry):
            return carry + tile_product(hidden[wide_index], down_tiles[narrow_index, wide_index], kept_slots[2, narrow_index, wide_index], kept_counts[2, narrow_index, wide_index], DT_DEV)
        return lax.fori_loop(0, N_WIDE, accumulate, jnp.zeros((TOKENS, DT_DEV, TILE), jnp.float32))
    out_sum = lax.map(out_block, jnp.arange(N_NARROW))
    layer_out = out_sum.transpose(1, 0, 2, 3).reshape(TOKENS, D).astype(jnp.bfloat16)

    def hidden_column(wide_index):

        def single(narrow_index):
            return tile_transposed(grad_blocks[narrow_index], down_tiles[narrow_index, wide_index], kept_slots[2, narrow_index, wide_index], kept_counts[2, narrow_index, wide_index], HT_DEV)
        return lax.optimization_barrier(jnp.sum(jax.vmap(single)(jnp.arange(N_NARROW)), 0))
    hidden_grad = lax.map(hidden_column, jnp.arange(N_WIDE))
    sigmoid_gate = jax.nn.sigmoid(gate_sum)
    gate_act = (hidden_grad * up_sum * sigmoid_gate * (1.0 + gate_sum * (1.0 - sigmoid_gate))).astype(jnp.bfloat16)
    up_act = (hidden_grad * gate_sum * sigmoid_gate).astype(jnp.bfloat16)

    def input_block(narrow_index):

        def accumulate(wide_index, carry):
            first = tile_transposed(gate_act[wide_index], gate_tiles[narrow_index, wide_index], kept_slots[0, narrow_index, wide_index], kept_counts[0, narrow_index, wide_index], DT_DEV)
            second = tile_transposed(up_act[wide_index], up_tiles[narrow_index, wide_index], kept_slots[1, narrow_index, wide_index], kept_counts[1, narrow_index, wide_index], DT_DEV)
            return carry + first + second
        return lax.fori_loop(0, N_WIDE, accumulate, jnp.zeros((TOKENS, DT_DEV, TILE), jnp.float32))
    input_sum = lax.map(input_block, jnp.arange(N_NARROW))
    input_grad = input_sum.transpose(1, 0, 2, 3).reshape(TOKENS, D).astype(jnp.bfloat16)

    def grad_row(narrow_index):

        def grad_cell(wide_index):
            first = tile_grad(token_blocks[narrow_index], gate_act[wide_index], kept_slots[0, narrow_index, wide_index], kept_counts[0, narrow_index, wide_index])
            second = tile_grad(token_blocks[narrow_index], up_act[wide_index], kept_slots[1, narrow_index, wide_index], kept_counts[1, narrow_index, wide_index])
            third = tile_grad(hidden[wide_index], grad_blocks[narrow_index], kept_slots[2, narrow_index, wide_index], kept_counts[2, narrow_index, wide_index])
            return (first, second, third)
        return lax.map(grad_cell, jnp.arange(N_WIDE))
    gate_grad, up_grad, down_grad = lax.map(grad_row, jnp.arange(N_NARROW))
    return (layer_out, input_grad, gate_grad, up_grad, down_grad)
```

```python
import functools

import jax
import jax.numpy as jnp
from jax import lax
from jax.experimental import pallas as pl
from jax.experimental.pallas import tpu as pltpu
from jax.sharding import PartitionSpec as P

HT = 3
VM = pl.BlockSpec(memory_space=pltpu.VMEM)
SM = pl.BlockSpec(memory_space=pltpu.SMEM)
ANY = pl.BlockSpec(memory_space=pl.ANY)
F32 = jnp.float32
BF16 = jnp.bfloat16


def group_of(cap):
    for size in (8, 6, 4, 3, 2):
        if cap % size == 0:
            return size
    return 1


def lanes(index, tile):
    return pl.ds(pl.multiple_of(index * tile, tile), tile)


def live_groups(count, group):
    return lax.div(count + (group - 1), group)


def forward_kernel(group, idx, counts, panel, gate, up, down, parts):
    tile = gate.shape[-1]
    rows = panel.shape[1]

    def stacked(which, m, base):
        blocks = []
        for j in range(group):
            k = base + j
            block = idx[m, 0, k]
            col = idx[m, 1, k]
            pick = panel[which, :, lanes(block, tile)]
            zero = jnp.zeros_like(pick)
            blocks.append(
                jnp.concatenate([jnp.where(col == c, pick, zero) for c in range(HT)], axis=0)
            )
        return jnp.concatenate(blocks, axis=1)

    for m, which, ref in ((0, 0, gate), (1, 0, up), (2, 1, down)):

        def step(g, acc, m=m, which=which, ref=ref):
            base = g * group
            lhs = stacked(which, m, base)
            if m < 2:
                rhs = ref[pl.ds(base, group)].reshape(group * tile, tile)
                return acc + lax.dot_general(
                    lhs, rhs, (((1,), (0,)), ((), ())), preferred_element_type=F32
                )
            rhs = jnp.concatenate([ref[base + j] for j in range(group)], axis=1)
            return acc + lax.dot_general(
                lhs, rhs, (((1,), (1,)), ((), ())), preferred_element_type=F32
            )

        total = lax.fori_loop(
            0, live_groups(counts[m], group), step, jnp.zeros((HT * rows, tile), F32)
        )
        parts[m] = total.reshape(HT, rows, tile)


def backward_kernel(
    group, quarters, idx, counts, parts, other, gate, up, down, acts, keep, *rest
):
    sends, (out_sum, in_sum) = rest[:quarters - 1], rest[quarters - 1:]
    tile = gate.shape[-1]
    rows = parts.shape[2]
    gate_sum = parts[0] + other[0]
    up_sum = parts[1] + other[1]
    hidden_grad = parts[2] + other[2]
    sig = jax.nn.sigmoid(gate_sum)
    acts[0, :HT] = (
        hidden_grad * up_sum * sig * (1.0 + gate_sum * (1.0 - sig))
    ).astype(BF16)
    acts[1, :HT] = (hidden_grad * gate_sum * sig).astype(BF16)
    acts[2, :HT] = (gate_sum * sig * up_sum).astype(BF16)
    for m in range(3):
        acts[m, HT] = jnp.zeros((rows, tile), BF16)
    out_sum[...] = jnp.zeros_like(out_sum)
    in_sum[...] = jnp.zeros_like(in_sum)
    for m, ref, target in ((2, down, out_sum), (0, gate, in_sum), (1, up, in_sum)):

        def step(g, carry, m=m, ref=ref, target=target):
            base = g * group
            products = []
            for j in range(group):
                lhs = acts[m, idx[m, 1, base + j]]
                dims = (((1,), (0 if m == 2 else 1,)), ((), ()))
                products.append(
                    lax.dot_general(lhs, ref[base + j], dims, preferred_element_type=F32)
                )
            for j in range(group):
                where = lanes(idx[m, 0, base + j], tile)
                target[:, where] += products[j]
            return carry

        lax.fori_loop(0, live_groups(counts[m], group), step, 0)
    size = rows // quarters
    for which, total in ((0, out_sum), (1, in_sum)):
        keep[which] = total[:size]
        for q in range(1, quarters):
            sends[q - 1][which] = total[q * size:(q + 1) * size].astype(BF16)


def grad_kernel(group, m, which, idx, counts, panel, acts, out, buf, sem):
    tile = out.shape[-1]
    cap = out.shape[0]
    copies = []
    for g in range(cap // group):
        for j in range(group):
            k = g * group + j
            block = panel[which, :, lanes(idx[m, 0, k], tile)]
            act = acts[m, idx[m, 1, k]]
            left, right = (act, block) if m == 2 else (block, act)
            buf[k] = lax.dot_general(
                left, right, (((0,), (0,)), ((), ())), preferred_element_type=F32
            ).astype(BF16)
        copy = pltpu.make_async_copy(
            buf.at[pl.ds(g * group, group)], out.at[pl.ds(g * group, group)], sem.at[g]
        )
        copy.start()
        copies.append(copy)
    for copy in copies:
        copy.wait()


def bits_of(size):
    assert size & (size - 1) == 0
    return [1 << i for i in range(size.bit_length() - 1)]


def per_device(tokens, cotangent, gate_tiles, up_tiles, down_tiles, kept_slots, kept_counts):
    tile = gate_tiles.shape[-1]
    cap = gate_tiles.shape[2]
    group = group_of(cap)
    feats = tokens.shape[1]
    row_blocks = feats // tile
    n_wide = lax.axis_size("wide")
    n_narrow = lax.axis_size("narrow")
    rows = tokens.shape[0] * n_wide
    bits = bits_of(n_wide)
    low, high = bits[:2], bits[2:][::-1]
    near = [sum(b for i, b in enumerate(low) if q >> i & 1) for q in range(1 << len(low))]
    quarters = len(near)

    def swap(x, bit, axis="wide"):
        size = lax.axis_size(axis)
        return lax.ppermute(x, axis, [(i, i ^ bit) for i in range(size)])

    slots = kept_slots[:, 0, 0]
    counts = kept_counts[:, 0, 0]
    live = jnp.arange(cap, dtype=jnp.int32)[None] < counts[:, None]
    is_down = jnp.arange(3)[:, None] == 2
    minor = jnp.where(is_down, row_blocks, HT)
    major_pos, minor_pos = slots // minor, slots % minor
    block = jnp.where(is_down, minor_pos, major_pos)
    column = jnp.where(live, jnp.where(is_down, major_pos, minor_pos), HT)
    idx = jnp.stack([block, column], axis=1)

    gate, up, down = gate_tiles[0, 0], up_tiles[0, 0], down_tiles[0, 0]

    held = jnp.stack([tokens, cotangent])
    for bit in high:
        held = jnp.concatenate([held, swap(held, bit)], axis=1)
    panel = jnp.concatenate(
        [held] + [swap(held, b) for b in near[1:]], axis=1
    )

    parts = pl.pallas_call(
        functools.partial(forward_kernel, group),
        out_shape=jax.ShapeDtypeStruct((3, HT, rows, tile), F32),
        in_specs=[SM, SM, VM, VM, VM, VM],
        out_specs=VM,
        name="forward",
    )(idx, counts, panel, gate, up, down)

    narrow_bits = bits_of(n_narrow)
    for bit in narrow_bits[:-1]:
        parts = parts + swap(parts, bit, "narrow")
    other = swap(parts, narrow_bits[-1], "narrow")

    size = rows // quarters
    acts, keep, *sends = pl.pallas_call(
        functools.partial(backward_kernel, group, quarters),
        out_shape=[
            jax.ShapeDtypeStruct((3, HT + 1, rows, tile), BF16),
            jax.ShapeDtypeStruct((2, size, feats), F32),
        ]
        + [jax.ShapeDtypeStruct((2, size, feats), BF16)] * (quarters - 1),
        in_specs=[SM, SM] + [VM] * 5,
        out_specs=[VM] * (quarters + 1),
        scratch_shapes=[pltpu.VMEM((rows, feats), F32)] * 2,
        name="backward",
    )(idx, counts, parts, other, gate, up, down)

    def tile_grads(m, which):
        return pl.pallas_call(
            functools.partial(grad_kernel, group, m, which),
            out_shape=jax.ShapeDtypeStruct((cap, tile, tile), BF16),
            in_specs=[SM, SM, VM, VM],
            out_specs=ANY,
            scratch_shapes=[
                pltpu.VMEM((cap, tile, tile), BF16),
                pltpu.SemaphoreType.DMA((cap // group,)),
            ],
            cost_estimate=pl.CostEstimate(
                flops=2 * cap * rows * tile * tile,
                bytes_accessed=4 * cap * tile * tile,
                transcendentals=0,
            ),
            name=f"grads{m}",
        )(idx, counts, panel, acts)

    got = [swap(s, b) for s, b in zip(sends, near[1:])]
    total = keep
    for g in got:
        total = total + g.astype(F32)
    for bit in high[::-1]:
        half = total.shape[1] // 2
        total = total[:, :half] + swap(total[:, half:].astype(BF16), bit).astype(F32)
    total = total.astype(BF16)
    grads = [tile_grads(m, w)[None, None] for m, w in ((0, 0), (1, 0), (2, 1))]
    return (total[0], total[1], *grads)


def solution(mesh):
    act = P("wide", "narrow")
    wts = P("narrow", "wide", None, None, None)
    in_specs = (act, act, wts, wts, wts, P(None, "narrow", "wide", None), P(None, "narrow", "wide"))
    out_specs = (act, act, wts, wts, wts)
    return jax.shard_map(
        per_device, mesh=mesh, in_specs=in_specs, out_specs=out_specs, check_vma=False
    )
```

```python
import functools

import jax
import jax.numpy as jnp
from jax import lax
from jax.experimental import pallas as pl
from jax.experimental.pallas import tpu as pltpu
from jax.sharding import PartitionSpec as P


HT = 3
VM = pl.BlockSpec(memory_space=pltpu.VMEM)
SM = pl.BlockSpec(memory_space=pltpu.SMEM)
HBM = pl.BlockSpec(memory_space=pltpu.HBM)
VLIM = pltpu.CompilerParams(vmem_limit_bytes=16 << 20)
F32 = jnp.float32
BF16 = jnp.bfloat16


def group_of(cap):
    for size in (8, 6, 4, 3, 2):
        if cap % size == 0:
            return size
    return 1


def lanes(index, tile):
    return pl.ds(pl.multiple_of(index * tile, tile), tile)


def live_groups(count, group):
    return lax.div(count + (group - 1), group)


def forward_kernel(group, idx, counts, panel, gate, up, down, parts):
    tile = gate.shape[-1]
    rows = panel.shape[1]

    def stacked(which, m, base):
        blocks = []
        for j in range(group):
            k = base + j
            block = idx[m, 0, k]
            col = idx[m, 1, k]
            pick = panel[which, :, lanes(block, tile)]
            zero = jnp.zeros_like(pick)
            blocks.append(
                jnp.concatenate([jnp.where(col == c, pick, zero) for c in range(HT)], axis=0)
            )
        return jnp.concatenate(blocks, axis=1)

    for m, which, ref in ((0, 0, gate), (1, 0, up), (2, 1, down)):

        def step(g, acc, m=m, which=which, ref=ref):
            base = g * group
            lhs = stacked(which, m, base)
            if m < 2:
                rhs = ref[pl.ds(base, group)].reshape(group * tile, tile)
                return acc + lax.dot_general(
                    lhs, rhs, (((1,), (0,)), ((), ())), preferred_element_type=F32
                )
            rhs = jnp.concatenate([ref[base + j] for j in range(group)], axis=1)
            return acc + lax.dot_general(
                lhs, rhs, (((1,), (1,)), ((), ())), preferred_element_type=F32
            )

        total = lax.fori_loop(
            0, live_groups(counts[m], group), step, jnp.zeros((HT * rows, tile), F32)
        )
        parts[m] = total.reshape(HT, rows, tile)


def backward_kernel(
    group, quarters, idx, counts, parts, other, gate, up, down, acts, keep, *rest
):
    sends, (out_sum, in_sum) = rest[:quarters - 1], rest[quarters - 1:]
    tile = gate.shape[-1]
    rows = parts.shape[2]
    gate_sum = parts[0] + other[0]
    up_sum = parts[1] + other[1]
    hidden_grad = parts[2] + other[2]
    sig = jax.nn.sigmoid(gate_sum)
    acts[0, :HT] = (
        hidden_grad * up_sum * sig * (1.0 + gate_sum * (1.0 - sig))
    ).astype(BF16)
    acts[1, :HT] = (hidden_grad * gate_sum * sig).astype(BF16)
    acts[2, :HT] = (gate_sum * sig * up_sum).astype(BF16)
    for m in range(3):
        acts[m, HT] = jnp.zeros((rows, tile), BF16)
    out_sum[...] = jnp.zeros_like(out_sum)
    in_sum[...] = jnp.zeros_like(in_sum)
    for m, ref, target in ((2, down, out_sum), (0, gate, in_sum), (1, up, in_sum)):

        def step(g, carry, m=m, ref=ref, target=target):
            base = g * group
            products = []
            for j in range(group):
                lhs = acts[m, idx[m, 1, base + j]]
                dims = (((1,), (0 if m == 2 else 1,)), ((), ()))
                products.append(
                    lax.dot_general(lhs, ref[base + j], dims, preferred_element_type=F32)
                )
            for j in range(group):
                where = lanes(idx[m, 0, base + j], tile)
                target[:, where] += products[j]
            return carry

        lax.fori_loop(0, live_groups(counts[m], group), step, 0)
    size = rows // quarters
    for which, total in ((0, out_sum), (1, in_sum)):
        keep[which] = total[:size]
        for q in range(1, quarters):
            sends[q - 1][which] = total[q * size:(q + 1) * size].astype(BF16)


def grad_kernel(group, m, which, idx, counts, panel, acts, out, buf, sem):
    tile = out.shape[-1]
    cap = out.shape[0]
    copies = []
    for g in range(cap // group):
        for j in range(group):
            k = g * group + j
            block = panel[which, :, lanes(idx[m, 0, k], tile)]
            act = acts[m, idx[m, 1, k]]
            left, right = (act, block) if m == 2 else (block, act)
            buf[k] = lax.dot_general(
                left, right, (((0,), (0,)), ((), ())), preferred_element_type=F32
            ).astype(BF16)
        copy = pltpu.make_async_copy(
            buf.at[pl.ds(g * group, group)], out.at[pl.ds(g * group, group)], sem.at[g]
        )
        copy.start()
        copies.append(copy)
    for copy in copies:
        copy.wait()


def load_kernel(gate_in, up_in, down_in, gate, up, down, sem):
    pairs = ((gate_in, gate), (up_in, up), (down_in, down))
    copies = [pltpu.make_async_copy(a, b, sem.at[i]) for i, (a, b) in enumerate(pairs)]
    for copy in copies:
        copy.start()
    for copy in copies:
        copy.wait()


def bits_of(size):
    assert size & (size - 1) == 0
    return [1 << i for i in range(size.bit_length() - 1)]


def stages_of(size):
    bits = bits_of(size)
    parts = [bits[i:i + 2] for i in range(0, len(bits), 2)]
    return [
        [sum(b for i, b in enumerate(part) if q >> i & 1) for q in range(1 << len(part))]
        for part in parts
    ]


def per_device(tokens, cotangent, gate_tiles, up_tiles, down_tiles, kept_slots, kept_counts):
    tile = gate_tiles.shape[-1]
    cap = gate_tiles.shape[2]
    group = group_of(cap)
    feats = tokens.shape[1]
    row_blocks = feats // tile
    n_wide = lax.axis_size("wide")
    n_narrow = lax.axis_size("narrow")
    rows = tokens.shape[0] * n_wide
    stages = stages_of(n_wide)
    quarters = len(stages[0])

    def swap(x, bit, axis="wide"):
        size = lax.axis_size(axis)
        return lax.ppermute(x, axis, [(i, i ^ bit) for i in range(size)])

    slots = kept_slots[:, 0, 0]
    counts = kept_counts[:, 0, 0]
    live = jnp.arange(cap, dtype=jnp.int32)[None] < counts[:, None]
    is_down = jnp.arange(3)[:, None] == 2
    minor = jnp.where(is_down, row_blocks, HT)
    major_pos, minor_pos = slots // minor, slots % minor
    block = jnp.where(is_down, minor_pos, major_pos)
    column = jnp.where(live, jnp.where(is_down, major_pos, minor_pos), HT)
    idx = jnp.stack([block, column], axis=1)

    gate, up, down = pl.pallas_call(
        load_kernel,
        out_shape=[pltpu.VMEM((cap, tile, tile), BF16)] * 3,
        in_specs=[HBM] * 3,
        out_specs=[VM] * 3,
        scratch_shapes=[pltpu.SemaphoreType.DMA((3,))],
        compiler_params=pltpu.CompilerParams(vmem_limit_bytes=58 << 20),
        name="load",
    )(gate_tiles[0, 0], up_tiles[0, 0], down_tiles[0, 0])

    held = lax.optimization_barrier(jnp.stack([tokens, cotangent]))
    for stage in stages[::-1]:
        pieces = [held] + [swap(held, offset) for offset in stage[1:]]
        held = lax.optimization_barrier(jnp.concatenate(pieces, axis=1))
    panel = held

    parts = pl.pallas_call(
        functools.partial(forward_kernel, group),
        out_shape=pltpu.VMEM((3, HT, rows, tile), F32),
        in_specs=[SM, SM, VM, VM, VM, VM],
        out_specs=VM,
        compiler_params=VLIM,
        name="forward",
    )(idx, counts, panel, gate, up, down)

    narrow_bits = bits_of(n_narrow)
    for bit in narrow_bits[:-1]:
        parts = parts + swap(parts, bit, "narrow")
    other = swap(parts, narrow_bits[-1], "narrow")

    size = rows // quarters
    acts, keep, *sends = pl.pallas_call(
        functools.partial(backward_kernel, group, quarters),
        out_shape=[
            jax.ShapeDtypeStruct((3, HT + 1, rows, tile), BF16),
            jax.ShapeDtypeStruct((2, size, feats), F32),
        ]
        + [jax.ShapeDtypeStruct((2, size, feats), BF16)] * (quarters - 1),
        in_specs=[SM, SM] + [VM] * 5,
        out_specs=[VM] * (quarters + 1),
        scratch_shapes=[pltpu.VMEM((rows, feats), F32)] * 2,
        compiler_params=VLIM,
        name="backward",
    )(idx, counts, parts, other, gate, up, down)

    def tile_grads(m, which):
        return pl.pallas_call(
            functools.partial(grad_kernel, group, m, which),
            out_shape=jax.ShapeDtypeStruct((cap, tile, tile), BF16),
            in_specs=[SM, SM, VM, VM],
            out_specs=HBM,
            scratch_shapes=[
                pltpu.VMEM((cap, tile, tile), BF16),
                pltpu.SemaphoreType.DMA((cap // group,)),
            ],
            cost_estimate=pl.CostEstimate(
                flops=2 * cap * rows * tile * tile,
                bytes_accessed=4 * cap * tile * tile,
                transcendentals=0,
            ),
            compiler_params=VLIM,
        )(idx, counts, panel, acts)

    got = [swap(s, offset) for s, offset in zip(sends, stages[0][1:])]
    total = keep
    for g in got:
        total = total + g.astype(F32)
    for stage in stages[1:]:
        size = total.shape[1] // len(stage)
        pieces = [total[:, q * size:(q + 1) * size] for q in range(len(stage))]
        total = pieces[0]
        for piece, offset in zip(pieces[1:], stage[1:]):
            total = total + swap(piece.astype(BF16), offset).astype(F32)
    total = total.astype(BF16)
    grads = [tile_grads(m, w)[None, None] for m, w in ((0, 0), (1, 0), (2, 1))]
    return (total[0], total[1], *grads)


def solution(mesh):
    act = P("wide", "narrow")
    wts = P("narrow", "wide", None, None, None)
    in_specs = (act, act, wts, wts, wts, P(None, "narrow", "wide", None), P(None, "narrow", "wide"))
    out_specs = (act, act, wts, wts, wts)
    return jax.shard_map(
        per_device, mesh=mesh, in_specs=in_specs, out_specs=out_specs, check_vma=False
    )
```

```python
import functools

import jax
import jax.numpy as jnp
from jax import lax
from jax.experimental import pallas as pl
from jax.experimental.pallas import tpu as pltpu
from jax.sharding import PartitionSpec as P


HT = 3
VM = pl.BlockSpec(memory_space=pltpu.VMEM)
SM = pl.BlockSpec(memory_space=pltpu.SMEM)
HBM = pl.BlockSpec(memory_space=pltpu.HBM)
VLIM = pltpu.CompilerParams(vmem_limit_bytes=16 << 20)
F32 = jnp.float32
BF16 = jnp.bfloat16


def group_of(cap):
    for size in (8, 6, 4, 2):
        if cap % size == 0:
            return size
    return 1


def lanes(index, tile):
    return pl.ds(pl.multiple_of(index * tile, tile), tile)


def forward_kernel(group, idx, panel, gate, up, down, parts):
    tile = gate.shape[-1]
    rows = panel.shape[1]

    def stacked(which, m, base):
        stack = []
        for j in range(group):
            k = base + j
            block = idx[m, 0, k]
            col = idx[m, 1, k]
            pick = panel[which, :, lanes(block, tile)]
            zero = jnp.zeros_like(pick)
            stack.append(
                jnp.concatenate([jnp.where(col == c, pick, zero) for c in range(HT)], axis=0)
            )
        return jnp.concatenate(stack, axis=1)

    def one(g, m, which, ref):
        base = g * group
        lhs = stacked(which, m, base)
        if m < 2:
            rhs = ref[pl.ds(base, group)].reshape(group * tile, tile)
            dims = (((1,), (0,)), ((), ()))
        else:
            rhs = jnp.concatenate([ref[base + j] for j in range(group)], axis=1)
            dims = (((1,), (1,)), ((), ()))
        return lax.dot_general(lhs, rhs, dims, preferred_element_type=F32)

    totals = [jnp.zeros((HT * rows, tile), F32)] * 3
    for g in range(gate.shape[0] // group):
        for m, which, ref in ((0, 0, gate), (1, 0, up), (2, 1, down)):
            totals[m] = totals[m] + one(g, m, which, ref)
    for m in range(3):
        parts[m] = totals[m].reshape(HT, rows, tile)


def backward_kernel(
    group, quarters, idx, parts, other, gate, up, down, acts, keep, *rest
):
    sends, (out_sum, in_sum) = rest[:quarters - 1], rest[quarters - 1:]
    tile = gate.shape[-1]
    rows = parts.shape[2]
    gate_sum = parts[0] + other[0]
    up_sum = parts[1] + other[1]
    hidden_grad = parts[2] + other[2]
    sig = jax.nn.sigmoid(gate_sum)
    acts[0, :HT] = (
        hidden_grad * up_sum * sig * (1.0 + gate_sum * (1.0 - sig))
    ).astype(BF16)
    acts[1, :HT] = (hidden_grad * gate_sum * sig).astype(BF16)
    acts[2, :HT] = (gate_sum * sig * up_sum).astype(BF16)
    for m in range(3):
        acts[m, HT] = jnp.zeros((rows, tile), BF16)
    out_sum[...] = jnp.zeros_like(out_sum)
    in_sum[...] = jnp.zeros_like(in_sum)
    blank = jnp.zeros((rows, tile), BF16)
    for g in range(gate.shape[0] // group):
        base = g * group
        for m, ref, target in ((2, down, out_sum), (0, gate, in_sum), (1, up, in_sum)):
            products = []
            for j in range(0, group, 2):
                k = base + j
                first, second = acts[m, idx[m, 1, k]], acts[m, idx[m, 1, k + 1]]
                lhs = jnp.concatenate(
                    [
                        jnp.concatenate([first, blank], axis=1),
                        jnp.concatenate([blank, second], axis=1),
                    ],
                    axis=0,
                )
                if m == 2:
                    rhs = ref[pl.ds(k, 2)].reshape(2 * tile, tile)
                    dims = (((1,), (0,)), ((), ()))
                else:
                    rhs = jnp.concatenate([ref[k], ref[k + 1]], axis=1)
                    dims = (((1,), (1,)), ((), ()))
                both = lax.dot_general(lhs, rhs, dims, preferred_element_type=F32)
                products += [both[:rows], both[rows:]]
            for j in range(group):
                where = lanes(idx[m, 0, base + j], tile)
                target[:, where] += products[j]
    size = rows // quarters
    for which, total in ((0, out_sum), (1, in_sum)):
        keep[which] = total[:size]
        for q in range(1, quarters):
            sends[q - 1][which] = total[q * size:(q + 1) * size].astype(BF16)


def grad_kernel(group, jobs, idx, panel, acts, *refs):
    outs, bufs, sem = refs[:len(jobs)], refs[len(jobs):-1], refs[-1]
    tile = outs[0].shape[-1]
    cap = outs[0].shape[0]
    copies = []
    for i, (m, which) in enumerate(jobs):
        for g in range(cap // group):
            for k in range(g * group, (g + 1) * group):
                block = panel[which, :, lanes(idx[m, 0, k], tile)]
                act = acts[m, idx[m, 1, k]]
                left, right = (act, block) if m == 2 else (block, act)
                bufs[i][k] = lax.dot_general(
                    left, right, (((0,), (0,)), ((), ())), preferred_element_type=F32
                ).astype(BF16)
            span = pl.ds(g * group, group)
            copy = pltpu.make_async_copy(bufs[i].at[span], outs[i].at[span], sem.at[i, g])
            copy.start()
            copies.append(copy)
    for copy in copies:
        copy.wait()


def load_kernel(gate_in, up_in, down_in, gate, up, down, sem):
    pairs = ((gate_in, gate), (up_in, up), (down_in, down))
    copies = [pltpu.make_async_copy(a, b, sem.at[i]) for i, (a, b) in enumerate(pairs)]
    for copy in copies:
        copy.start()
    for copy in copies:
        copy.wait()


def bits_of(size):
    assert size & (size - 1) == 0
    return [1 << i for i in range(size.bit_length() - 1)]


def stages_of(size):
    bits = bits_of(size)
    parts = [bits[i:i + 2] for i in range(0, len(bits), 2)]
    return [
        [sum(b for i, b in enumerate(part) if q >> i & 1) for q in range(1 << len(part))]
        for part in parts
    ]


def per_device(tokens, cotangent, gate_tiles, up_tiles, down_tiles, kept_slots, kept_counts):
    tile = gate_tiles.shape[-1]
    cap = gate_tiles.shape[2]
    group = group_of(cap)
    feats = tokens.shape[1]
    row_blocks = feats // tile
    n_wide = lax.axis_size("wide")
    n_narrow = lax.axis_size("narrow")
    rows = tokens.shape[0] * n_wide
    stages = stages_of(n_wide)
    quarters = len(stages[0])

    def swap(x, bit, axis="wide"):
        size = lax.axis_size(axis)
        return lax.ppermute(x, axis, [(i, i ^ bit) for i in range(size)])

    slots = kept_slots[:, 0, 0]
    counts = kept_counts[:, 0, 0]
    live = jnp.arange(cap, dtype=jnp.int32)[None] < counts[:, None]
    is_down = jnp.arange(3)[:, None] == 2
    minor = jnp.where(is_down, row_blocks, HT)
    major_pos, minor_pos = slots // minor, slots % minor
    block = jnp.where(is_down, minor_pos, major_pos)
    column = jnp.where(live, jnp.where(is_down, major_pos, minor_pos), HT)
    idx = jnp.stack([block, column], axis=1)

    gate, up, down = pl.pallas_call(
        load_kernel,
        out_shape=[pltpu.VMEM((cap, tile, tile), BF16)] * 3,
        in_specs=[HBM] * 3,
        out_specs=[VM] * 3,
        scratch_shapes=[pltpu.SemaphoreType.DMA((3,))],
        compiler_params=pltpu.CompilerParams(vmem_limit_bytes=58 << 20),
        name="load",
    )(gate_tiles[0, 0], up_tiles[0, 0], down_tiles[0, 0])

    held = lax.optimization_barrier(jnp.stack([tokens, cotangent]))
    for stage in stages[::-1]:
        pieces = [held] + [swap(held, offset) for offset in stage[1:]]
        held = lax.optimization_barrier(jnp.concatenate(pieces, axis=1))
    panel = held

    parts = pl.pallas_call(
        functools.partial(forward_kernel, group),
        out_shape=pltpu.VMEM((3, HT, rows, tile), F32),
        in_specs=[SM, VM, VM, VM, VM],
        out_specs=VM,
        compiler_params=VLIM,
        name="forward",
    )(idx, panel, gate, up, down)

    narrow_bits = bits_of(n_narrow)
    for bit in narrow_bits[:-1]:
        parts = parts + swap(parts, bit, "narrow")
    other = swap(parts, narrow_bits[-1], "narrow")

    size = rows // quarters
    acts, keep, *sends = pl.pallas_call(
        functools.partial(backward_kernel, group, quarters),
        out_shape=[
            jax.ShapeDtypeStruct((3, HT + 1, rows, tile), BF16),
            jax.ShapeDtypeStruct((2, size, feats), F32),
        ]
        + [jax.ShapeDtypeStruct((2, size, feats), BF16)] * (quarters - 1),
        in_specs=[SM] + [VM] * 5,
        out_specs=[VM] * (quarters + 1),
        scratch_shapes=[pltpu.VMEM((rows, feats), F32)] * 2,
        compiler_params=VLIM,
        name="backward",
    )(idx, parts, other, gate, up, down)

    def tile_grads(jobs):
        return pl.pallas_call(
            functools.partial(grad_kernel, group, jobs),
            out_shape=[jax.ShapeDtypeStruct((cap, tile, tile), BF16)] * len(jobs),
            in_specs=[SM, VM, VM],
            out_specs=[HBM] * len(jobs),
            scratch_shapes=[pltpu.VMEM((cap, tile, tile), BF16)] * len(jobs)
            + [pltpu.SemaphoreType.DMA((len(jobs), cap // group))],
            cost_estimate=pl.CostEstimate(
                flops=len(jobs) * 2 * cap * rows * tile * tile,
                bytes_accessed=len(jobs) * 4 * cap * tile * tile,
                transcendentals=0,
            ),
            compiler_params=VLIM,
        )(idx, panel, acts)

    got = [swap(s, offset) for s, offset in zip(sends, stages[0][1:])]
    total = keep
    for g in got:
        total = total + g.astype(F32)
    for stage in stages[1:]:
        size = total.shape[1] // len(stage)
        pieces = [total[:, q * size:(q + 1) * size] for q in range(len(stage))]
        total = pieces[0]
        for piece, offset in zip(pieces[1:], stage[1:]):
            total = total + swap(piece.astype(BF16), offset).astype(F32)
    total = total.astype(BF16)
    gate_grad, up_grad, down_grad = tile_grads(((0, 0), (1, 0), (2, 1)))
    grads = [g[None, None] for g in (gate_grad, up_grad, down_grad)]
    return (total[0], total[1], *grads)


def solution(mesh):
    act = P("wide", "narrow")
    wts = P("narrow", "wide", None, None, None)
    in_specs = (act, act, wts, wts, wts, P(None, "narrow", "wide", None), P(None, "narrow", "wide"))
    out_specs = (act, act, wts, wts, wts)
    return jax.shard_map(
        per_device, mesh=mesh, in_specs=in_specs, out_specs=out_specs, check_vma=False
    )
```

```python
import functools

import jax
import jax.numpy as jnp
from jax import lax
from jax.experimental import pallas as pl
from jax.experimental.pallas import tpu as pltpu
from jax.sharding import PartitionSpec as P


HT = 3
THIRD = 43691
VM = pl.BlockSpec(memory_space=pltpu.VMEM)
SM = pl.BlockSpec(memory_space=pltpu.SMEM)
HBM = pl.BlockSpec(memory_space=pltpu.HBM)
VLIM = pltpu.CompilerParams(vmem_limit_bytes=16 << 20)
F32 = jnp.float32
BF16 = jnp.bfloat16


def group_of(cap):
    for size in (8, 6, 4, 2):
        if cap % size == 0:
            return size
    return 1


def lanes(index, tile):
    return pl.ds(pl.multiple_of(index * tile, tile), tile)


def rows_of(panel_a, panel_b, which, block, tile):
    where = lanes(block, tile)
    return jnp.concatenate([panel_a[which, :, where], panel_b[which, :, where]], axis=0)


def forward_kernel(group, idx, panel_a, panel_b, gate, up, down, parts):
    tile = gate.shape[-1]
    rows = panel_a.shape[1] + panel_b.shape[1]

    def stacked(which, m, base):
        stack = []
        for j in range(group):
            k = base + j
            block = idx[m, 0, k]
            col = idx[m, 1, k]
            pick = rows_of(panel_a, panel_b, which, block, tile)
            zero = jnp.zeros_like(pick)
            stack.append(
                jnp.concatenate([jnp.where(col == c, pick, zero) for c in range(HT)], axis=0)
            )
        return jnp.concatenate(stack, axis=1)

    def one(g, m, which, ref):
        base = g * group
        lhs = stacked(which, m, base)
        if m < 2:
            rhs = ref[pl.ds(base, group)].reshape(group * tile, tile)
            dims = (((1,), (0,)), ((), ()))
        else:
            rhs = jnp.concatenate([ref[base + j] for j in range(group)], axis=1)
            dims = (((1,), (1,)), ((), ()))
        return lax.dot_general(lhs, rhs, dims, preferred_element_type=F32)

    totals = [jnp.zeros((HT * rows, tile), F32)] * 3
    for g in range(gate.shape[0] // group):
        for m, which, ref in ((0, 0, gate), (1, 0, up), (2, 1, down)):
            totals[m] = totals[m] + one(g, m, which, ref)
    for m in range(3):
        parts[m] = totals[m].reshape(HT, rows, tile)


def backward_kernel(
    group, quarters, idx, parts, other, gate, up, down, acts, *rest
):
    keeps, sends, (out_sum, in_sum) = rest[:2], rest[2:-2], rest[-2:]
    tile = gate.shape[-1]
    rows = parts.shape[2]
    gate_sum = parts[0] + other[0]
    up_sum = parts[1] + other[1]
    hidden_grad = parts[2] + other[2]
    sig = jax.nn.sigmoid(gate_sum)
    acts[0, :HT] = (
        hidden_grad * up_sum * sig * (1.0 + gate_sum * (1.0 - sig))
    ).astype(BF16)
    acts[1, :HT] = (hidden_grad * gate_sum * sig).astype(BF16)
    acts[2, :HT] = (gate_sum * sig * up_sum).astype(BF16)
    for m in range(3):
        acts[m, HT] = jnp.zeros((rows, tile), BF16)
    out_sum[...] = jnp.zeros_like(out_sum)
    in_sum[...] = jnp.zeros_like(in_sum)
    blank = jnp.zeros((rows, tile), BF16)
    for g in range(gate.shape[0] // group):
        base = g * group
        for m, ref, target in ((2, down, out_sum), (0, gate, in_sum), (1, up, in_sum)):
            products = []
            for j in range(0, group, 2):
                k = base + j
                first, second = acts[m, idx[m, 1, k]], acts[m, idx[m, 1, k + 1]]
                lhs = jnp.concatenate(
                    [
                        jnp.concatenate([first, blank], axis=1),
                        jnp.concatenate([blank, second], axis=1),
                    ],
                    axis=0,
                )
                if m == 2:
                    rhs = ref[pl.ds(k, 2)].reshape(2 * tile, tile)
                    dims = (((1,), (0,)), ((), ()))
                else:
                    rhs = jnp.concatenate([ref[k], ref[k + 1]], axis=1)
                    dims = (((1,), (1,)), ((), ()))
                both = lax.dot_general(lhs, rhs, dims, preferred_element_type=F32)
                products += [both[:rows], both[rows:]]
            for j in range(group):
                where = lanes(idx[m, 0, base + j], tile)
                target[:, where] += products[j]
    size = rows // (2 * quarters)
    for h in range(2):
        for q in range(quarters):
            span = pl.ds((h * quarters + q) * size, size)
            for which, total in ((0, out_sum), (1, in_sum)):
                if q == 0:
                    keeps[h][which] = total[span]
                else:
                    sends[h * (quarters - 1) + q - 1][which] = total[span].astype(BF16)


def grad_kernel(group, jobs, idx, panel_a, panel_b, acts, *refs):
    outs, bufs, sem = refs[:len(jobs)], refs[len(jobs):-1], refs[-1]
    tile = outs[0].shape[-1]
    cap = outs[0].shape[0]
    copies = []
    for i, (m, which) in enumerate(jobs):
        for g in range(cap // group):
            for k in range(g * group, (g + 1) * group):
                block = rows_of(panel_a, panel_b, which, idx[m, 0, k], tile)
                act = acts[m, idx[m, 1, k]]
                left, right = (act, block) if m == 2 else (block, act)
                bufs[i][k] = lax.dot_general(
                    left, right, (((0,), (0,)), ((), ())), preferred_element_type=F32
                ).astype(BF16)
            span = pl.ds(g * group, group)
            copy = pltpu.make_async_copy(bufs[i].at[span], outs[i].at[span], sem.at[i, g])
            copy.start()
            copies.append(copy)
    for copy in copies:
        copy.wait()


def load_kernel(
    row_blocks, slots_in, counts_in, gate_in, up_in, down_in, gate, up, down, idx, slots, counts, sem
):
    pairs = (
        (slots_in, slots),
        (counts_in, counts),
        (gate_in, gate),
        (up_in, up),
        (down_in, down),
    )
    copies = [pltpu.make_async_copy(a, b, sem.at[i]) for i, (a, b) in enumerate(pairs)]
    for copy in copies:
        copy.start()
    for copy in copies[:2]:
        copy.wait()
    for m in range(3):
        spot = slots[m]
        if m == 2:
            column = sum((spot >= c * row_blocks).astype(jnp.int32) for c in range(1, HT))
            block = spot - column * row_blocks
        else:
            block = lax.shift_right_logical(spot * THIRD, 17)
            column = spot - block * HT
        order = lax.broadcasted_iota(jnp.int32, spot.shape, 1)
        idx[m, 0:1] = block
        idx[m, 1:2] = jnp.where(order < counts[m], column, HT)
    for copy in copies[2:]:
        copy.wait()


def bits_of(size):
    assert size & (size - 1) == 0
    return [1 << i for i in range(size.bit_length() - 1)]


def stages_of(size):
    bits = bits_of(size)
    parts = [bits[i:i + 2] for i in range(0, len(bits), 2)]
    return [
        [sum(b for i, b in enumerate(part) if q >> i & 1) for q in range(1 << len(part))]
        for part in parts
    ]


def per_device(tokens, cotangent, gate_tiles, up_tiles, down_tiles, kept_slots, kept_counts):
    tile = gate_tiles.shape[-1]
    cap = gate_tiles.shape[2]
    group = group_of(cap)
    feats = tokens.shape[1]
    row_blocks = feats // tile
    n_wide = lax.axis_size("wide")
    n_narrow = lax.axis_size("narrow")
    rows = tokens.shape[0] * n_wide
    stages = stages_of(n_wide)
    quarters = len(stages[0])

    def swap(x, bit, axis="wide"):
        size = lax.axis_size(axis)
        return lax.ppermute(x, axis, [(i, i ^ bit) for i in range(size)])

    gate, up, down, idx = pl.pallas_call(
        functools.partial(load_kernel, row_blocks),
        out_shape=[pltpu.VMEM((cap, tile, tile), BF16)] * 3
        + [pltpu.VMEM((3, 2, cap), jnp.int32)],
        in_specs=[HBM] * 5,
        out_specs=[VM] * 4,
        scratch_shapes=[
            pltpu.VMEM((3, 1, cap), jnp.int32),
            pltpu.SMEM((3,), jnp.int32),
            pltpu.SemaphoreType.DMA((5,)),
        ],
        compiler_params=pltpu.CompilerParams(vmem_limit_bytes=57 << 20),
        name="load",
    )(kept_slots[:, 0], kept_counts[:, 0, 0], gate_tiles[0, 0], up_tiles[0, 0], down_tiles[0, 0])

    held = lax.optimization_barrier(jnp.stack([tokens, cotangent]))
    for stage in stages[:1:-1]:
        pieces = [held] + [swap(held, offset) for offset in stage[1:]]
        held = lax.optimization_barrier(jnp.concatenate(pieces, axis=1))
    pieces = [held] + [swap(held, offset) for offset in stages[1][1:]]
    half = len(pieces) // 2
    halves = []
    for part in (pieces[:half], pieces[half:]):
        halves.append(lax.optimization_barrier(jnp.concatenate(part, axis=1)))
    quarter_rows = [[part] + [swap(part, offset) for offset in stages[0][1:]] for part in halves]
    panels = [lax.optimization_barrier(jnp.concatenate(part, axis=1)) for part in quarter_rows]

    parts = pl.pallas_call(
        functools.partial(forward_kernel, group),
        out_shape=pltpu.VMEM((3, HT, rows, tile), F32),
        in_specs=[SM] + [VM] * 5,
        out_specs=VM,
        compiler_params=VLIM,
        name="forward",
    )(idx, *panels, gate, up, down)

    narrow_bits = bits_of(n_narrow)
    for bit in narrow_bits[:-1]:
        parts = parts + swap(parts, bit, "narrow")
    other = swap(parts, narrow_bits[-1], "narrow")

    size = rows // (2 * quarters)
    acts, *moved = pl.pallas_call(
        functools.partial(backward_kernel, group, quarters),
        out_shape=[jax.ShapeDtypeStruct((3, HT + 1, rows, tile), BF16)]
        + [jax.ShapeDtypeStruct((2, size, feats), F32)] * 2
        + [jax.ShapeDtypeStruct((2, size, feats), BF16)] * (2 * quarters - 2),
        in_specs=[SM] + [VM] * 5,
        out_specs=[VM] * (2 * quarters + 1),
        scratch_shapes=[pltpu.VMEM((rows, feats), F32)] * 2,
        compiler_params=VLIM,
        name="backward",
    )(idx, parts, other, gate, up, down)
    keeps, sends = moved[:2], [moved[2:quarters + 1], moved[quarters + 1:]]

    def tile_grads(jobs):
        return pl.pallas_call(
            functools.partial(grad_kernel, group, jobs),
            out_shape=[jax.ShapeDtypeStruct((cap, tile, tile), BF16)] * len(jobs),
            in_specs=[SM, VM, VM, VM],
            out_specs=[HBM] * len(jobs),
            scratch_shapes=[pltpu.VMEM((cap, tile, tile), BF16)] * len(jobs)
            + [pltpu.SemaphoreType.DMA((len(jobs), cap // group))],
            cost_estimate=pl.CostEstimate(
                flops=len(jobs) * 2 * cap * rows * tile * tile,
                bytes_accessed=len(jobs) * 4 * cap * tile * tile,
                transcendentals=0,
            ),
            compiler_params=VLIM,
        )(idx, *panels, acts)

    got = {h: [swap(s, offset) for s, offset in zip(sends[h], stages[0][1:])] for h in (1, 0)}
    blocks = {}
    for h in (1, 0):
        total = keeps[h]
        for g in got[h]:
            total = total + g.astype(F32)
        count = len(stages[1]) // 2
        step = size // count
        for i in range(count):
            blocks[h * count + i] = total[:, i * step:(i + 1) * step]
            if h * count + i:
                blocks[h * count + i] = blocks[h * count + i].astype(BF16)
    total = blocks[0]
    for i, offset in enumerate(stages[1][1:], 1):
        total = total + swap(blocks[i], offset).astype(F32)
    for stage in stages[2:]:
        size = total.shape[1] // len(stage)
        pieces = [total[:, q * size:(q + 1) * size] for q in range(len(stage))]
        total = pieces[0]
        for piece, offset in zip(pieces[1:], stage[1:]):
            total = total + swap(piece.astype(BF16), offset).astype(F32)
    total = total.astype(BF16)
    gate_grad, up_grad, down_grad = tile_grads(((0, 0), (1, 0), (2, 1)))
    grads = [g[None, None] for g in (gate_grad, up_grad, down_grad)]
    return (total[0], total[1], *grads)


def solution(mesh):
    act = P("wide", "narrow")
    wts = P("narrow", "wide", None, None, None)
    in_specs = (act, act, wts, wts, wts, P(None, "narrow", "wide", None), P(None, "narrow", "wide"))
    out_specs = (act, act, wts, wts, wts)
    return jax.shard_map(
        per_device, mesh=mesh, in_specs=in_specs, out_specs=out_specs, check_vma=False
    )
```

```python
import functools

import jax
import jax.numpy as jnp
from jax import lax
from jax.experimental import pallas as pl
from jax.experimental.pallas import tpu as pltpu
from jax.sharding import PartitionSpec as P


HT = 3
THIRD = 43691
VM = pl.BlockSpec(memory_space=pltpu.VMEM)
SM = pl.BlockSpec(memory_space=pltpu.SMEM)
HBM = pl.BlockSpec(memory_space=pltpu.HBM)
VLIM = pltpu.CompilerParams(vmem_limit_bytes=16 << 20)
F32 = jnp.float32
BF16 = jnp.bfloat16


def group_of(cap):
    for size in (8, 6, 4, 2):
        if cap % size == 0:
            return size
    return 1


def lanes(index, tile):
    return pl.ds(pl.multiple_of(index * tile, tile), tile)


def rows_of(panel_a, panel_b, which, block, tile):
    where = lanes(block, tile)
    return jnp.concatenate([panel_a[which, :, where], panel_b[which, :, where]], axis=0)


def forward_kernel(group, idx, panel_a, panel_b, gate, up, down, parts):
    tile = gate.shape[-1]
    rows = panel_a.shape[1] + panel_b.shape[1]

    def stacked(which, m, base):
        stack = []
        for j in range(group):
            k = base + j
            block = idx[m, 0, k]
            col = idx[m, 1, k]
            pick = rows_of(panel_a, panel_b, which, block, tile)
            zero = jnp.zeros_like(pick)
            stack.append(
                jnp.concatenate([jnp.where(col == c, pick, zero) for c in range(HT)], axis=0)
            )
        return jnp.concatenate(stack, axis=1)

    def one(g, m, which, ref):
        base = g * group
        lhs = stacked(which, m, base)
        if m < 2:
            rhs = ref[pl.ds(base, group)].reshape(group * tile, tile)
            dims = (((1,), (0,)), ((), ()))
        else:
            rhs = jnp.concatenate([ref[base + j] for j in range(group)], axis=1)
            dims = (((1,), (1,)), ((), ()))
        return lax.dot_general(lhs, rhs, dims, preferred_element_type=F32)

    totals = [jnp.zeros((HT * rows, tile), F32)] * 3
    for g in range(gate.shape[0] // group):
        for m, which, ref in ((0, 0, gate), (1, 0, up), (2, 1, down)):
            totals[m] = totals[m] + one(g, m, which, ref)
    for m in range(3):
        parts[m] = totals[m].reshape(HT, rows, tile)


def backward_kernel(
    group, quarters, idx, parts, other, gate, up, down, acts, *rest
):
    keeps, sends, (out_sum, in_sum) = rest[:2], rest[2:-2], rest[-2:]
    tile = gate.shape[-1]
    rows = parts.shape[2]
    gate_sum = parts[0] + other[0]
    up_sum = parts[1] + other[1]
    hidden_grad = parts[2] + other[2]
    sig = jax.nn.sigmoid(gate_sum)
    acts[0, :HT] = (
        hidden_grad * up_sum * sig * (1.0 + gate_sum * (1.0 - sig))
    ).astype(BF16)
    acts[1, :HT] = (hidden_grad * gate_sum * sig).astype(BF16)
    acts[2, :HT] = (gate_sum * sig * up_sum).astype(BF16)
    for m in range(3):
        acts[m, HT] = jnp.zeros((rows, tile), BF16)
    out_sum[...] = jnp.zeros_like(out_sum)
    in_sum[...] = jnp.zeros_like(in_sum)
    blank = jnp.zeros((rows, tile), BF16)
    for g in range(gate.shape[0] // group):
        base = g * group
        for m, ref, target in ((2, down, out_sum), (0, gate, in_sum), (1, up, in_sum)):
            products = []
            for j in range(0, group, 2):
                k = base + j
                first, second = acts[m, idx[m, 1, k]], acts[m, idx[m, 1, k + 1]]
                lhs = jnp.concatenate(
                    [
                        jnp.concatenate([first, blank], axis=1),
                        jnp.concatenate([blank, second], axis=1),
                    ],
                    axis=0,
                )
                if m == 2:
                    rhs = ref[pl.ds(k, 2)].reshape(2 * tile, tile)
                    dims = (((1,), (0,)), ((), ()))
                else:
                    rhs = jnp.concatenate([ref[k], ref[k + 1]], axis=1)
                    dims = (((1,), (1,)), ((), ()))
                both = lax.dot_general(lhs, rhs, dims, preferred_element_type=F32)
                products += [both[:rows], both[rows:]]
            for j in range(group):
                where = lanes(idx[m, 0, base + j], tile)
                target[:, where] += products[j]
    size = rows // (2 * quarters)
    for h in range(2):
        for q in range(quarters):
            span = pl.ds((h * quarters + q) * size, size)
            for which, total in ((0, out_sum), (1, in_sum)):
                if q == 0:
                    keeps[h][which] = total[span]
                else:
                    sends[h * (quarters - 1) + q - 1][which] = total[span].astype(BF16)


def grad_kernel(group, jobs, idx, panel_a, panel_b, acts, *refs):
    outs, bufs, sem = refs[:len(jobs)], refs[len(jobs):-1], refs[-1]
    tile = outs[0].shape[-1]
    cap = outs[0].shape[0]
    copies = []
    for i, (m, which) in enumerate(jobs):
        for g in range(cap // group):
            for k in range(g * group, (g + 1) * group):
                block = rows_of(panel_a, panel_b, which, idx[m, 0, k], tile)
                act = acts[m, idx[m, 1, k]]
                left, right = (act, block) if m == 2 else (block, act)
                bufs[i][k] = lax.dot_general(
                    left, right, (((0,), (0,)), ((), ())), preferred_element_type=F32
                ).astype(BF16)
            span = pl.ds(g * group, group)
            copy = pltpu.make_async_copy(bufs[i].at[span], outs[i].at[span], sem.at[i, g])
            copy.start()
            copies.append(copy)
    for copy in copies:
        copy.wait()


def load_kernel(
    row_blocks, slots_in, counts_in, gate_in, up_in, down_in, gate, up, down, idx, slots, counts, sem
):
    pairs = (
        (slots_in, slots),
        (counts_in, counts),
        (gate_in, gate),
        (up_in, up),
        (down_in, down),
    )
    copies = [pltpu.make_async_copy(a, b, sem.at[i]) for i, (a, b) in enumerate(pairs)]
    for copy in copies:
        copy.start()
    for copy in copies[:2]:
        copy.wait()
    for m in range(3):
        spot = slots[m]
        if m == 2:
            column = sum((spot >= c * row_blocks).astype(jnp.int32) for c in range(1, HT))
            block = spot - column * row_blocks
        else:
            block = lax.shift_right_logical(spot * THIRD, 17)
            column = spot - block * HT
        order = lax.broadcasted_iota(jnp.int32, spot.shape, 1)
        idx[m, 0:1] = block
        idx[m, 1:2] = jnp.where(order < counts[m], column, HT)
    for copy in copies[2:]:
        copy.wait()


def bits_of(size):
    assert size & (size - 1) == 0
    return [1 << i for i in range(size.bit_length() - 1)]


def stages_of(size):
    bits = bits_of(size)
    parts = [bits[i:i + 2] for i in range(0, len(bits), 2)]
    return [
        [sum(b for i, b in enumerate(part) if q >> i & 1) for q in range(1 << len(part))]
        for part in parts
    ]


def per_device(tokens, cotangent, gate_tiles, up_tiles, down_tiles, kept_slots, kept_counts):
    tile = gate_tiles.shape[-1]
    cap = gate_tiles.shape[2]
    group = group_of(cap)
    feats = tokens.shape[1]
    row_blocks = feats // tile
    n_wide = lax.axis_size("wide")
    n_narrow = lax.axis_size("narrow")
    rows = tokens.shape[0] * n_wide
    stages = stages_of(n_wide)
    quarters = len(stages[0])

    def swap(x, bit, axis="wide"):
        size = lax.axis_size(axis)
        return lax.ppermute(x, axis, [(i, i ^ bit) for i in range(size)])

    gate, up, down, idx = pl.pallas_call(
        functools.partial(load_kernel, row_blocks),
        out_shape=[pltpu.VMEM((cap, tile, tile), BF16)] * 3
        + [pltpu.VMEM((3, 2, cap), jnp.int32)],
        in_specs=[HBM] * 5,
        out_specs=[VM] * 4,
        scratch_shapes=[
            pltpu.VMEM((3, 1, cap), jnp.int32),
            pltpu.SMEM((3,), jnp.int32),
            pltpu.SemaphoreType.DMA((5,)),
        ],
        compiler_params=pltpu.CompilerParams(vmem_limit_bytes=57 << 20),
        name="load",
    )(kept_slots[:, 0], kept_counts[:, 0, 0], gate_tiles[0, 0], up_tiles[0, 0], down_tiles[0, 0])

    held = lax.optimization_barrier(jnp.stack([tokens, cotangent]))
    for stage in stages[:1:-1]:
        pieces = [held] + [swap(held, offset) for offset in stage[1:]]
        held = lax.optimization_barrier(jnp.concatenate(pieces, axis=1))
    pieces = [held] + [swap(held, offset) for offset in stages[1][1:]]
    half = len(pieces) // 2
    halves = []
    for part in (pieces[:half], pieces[half:]):
        halves.append(lax.optimization_barrier(jnp.concatenate(part, axis=1)))
    quarter_rows = [[part] + [swap(part, offset) for offset in stages[0][1:]] for part in halves]
    panels = []
    for part in quarter_rows:
        panels.append(lax.optimization_barrier(jnp.concatenate(part, axis=1)))

    parts = pl.pallas_call(
        functools.partial(forward_kernel, group),
        out_shape=pltpu.VMEM((3, HT, rows, tile), F32),
        in_specs=[SM] + [VM] * 5,
        out_specs=VM,
        compiler_params=VLIM,
        name="forward",
    )(idx, *panels, gate, up, down)

    narrow_bits = bits_of(n_narrow)
    for bit in narrow_bits[:-1]:
        parts = parts + swap(parts, bit, "narrow")
    other = swap(parts, narrow_bits[-1], "narrow")

    size = rows // (2 * quarters)
    acts, *moved = pl.pallas_call(
        functools.partial(backward_kernel, group, quarters),
        out_shape=[jax.ShapeDtypeStruct((3, HT + 1, rows, tile), BF16)]
        + [jax.ShapeDtypeStruct((2, size, feats), F32)] * 2
        + [jax.ShapeDtypeStruct((2, size, feats), BF16)] * (2 * quarters - 2),
        in_specs=[SM] + [VM] * 5,
        out_specs=[VM] * (2 * quarters + 1),
        scratch_shapes=[pltpu.VMEM((rows, feats), F32)] * 2,
        compiler_params=VLIM,
        name="backward",
    )(idx, parts, other, gate, up, down)
    keeps, sends = moved[:2], [moved[2:quarters + 1], moved[quarters + 1:]]

    def tile_grads(jobs):
        return pl.pallas_call(
            functools.partial(grad_kernel, group, jobs),
            out_shape=[jax.ShapeDtypeStruct((cap, tile, tile), BF16)] * len(jobs),
            in_specs=[SM, VM, VM, VM],
            out_specs=[HBM] * len(jobs),
            scratch_shapes=[pltpu.VMEM((cap, tile, tile), BF16)] * len(jobs)
            + [pltpu.SemaphoreType.DMA((len(jobs), cap // group))],
            cost_estimate=pl.CostEstimate(
                flops=len(jobs) * 2 * cap * rows * tile * tile,
                bytes_accessed=len(jobs) * 4 * cap * tile * tile,
                transcendentals=0,
            ),
            compiler_params=VLIM,
        )(idx, *panels, acts)

    got = {h: [swap(s, offset) for s, offset in zip(sends[h], stages[0][1:])] for h in (1, 0)}
    blocks = {}
    for h in (1, 0):
        total = keeps[h]
        for g in got[h]:
            total = total + g.astype(F32)
        count = len(stages[1]) // 2
        step = size // count
        for i in range(count):
            blocks[h * count + i] = total[:, i * step:(i + 1) * step]
            if h * count + i:
                blocks[h * count + i] = blocks[h * count + i].astype(BF16)
    pieces = [blocks[i] for i in range(len(stages[1]))]
    for stage, following in zip(stages[1:], stages[2:] + [None]):
        came = [swap(piece.astype(BF16), offset) for piece, offset in zip(pieces[1:], stage[1:])]
        sums = [sum((c[w].astype(F32) for c in came), pieces[0][w]) for w in range(2)]
        if following:
            total = jnp.stack(sums)
            size = total.shape[1] // len(following)
            pieces = [total[:, q * size:(q + 1) * size] for q in range(len(following))]
    layer_out, input_grad = [value.astype(BF16) for value in sums]
    gate_grad, up_grad, down_grad = tile_grads(((0, 0), (1, 0), (2, 1)))
    grads = [g[None, None] for g in (gate_grad, up_grad, down_grad)]
    return (layer_out, input_grad, *grads)


def solution(mesh):
    act = P("wide", "narrow")
    wts = P("narrow", "wide", None, None, None)
    in_specs = (act, act, wts, wts, wts, P(None, "narrow", "wide", None), P(None, "narrow", "wide"))
    out_specs = (act, act, wts, wts, wts)
    return jax.shard_map(
        per_device, mesh=mesh, in_specs=in_specs, out_specs=out_specs, check_vma=False
    )
```
